1024 devices in a mesh: mem: 64 (over z, x), lat: 2 (over y_hi), lon: 8 (over y_lo, core).
Axes of the slice: x: 8, y: 8 (y_hi: 2, y_lo: 4; y = y_hi * 4 + y_lo), z: 8, core: 2. Of those that a mesh axis runs over, the one named last changes fastest.
Arguments:
- members: bfloat16 [128, 16, 256, 512], P('mem', None, 'lon', 'lat'), may hold values from -16 to 16
- control_fine: bfloat16 [128, 16, 256, 512], P('mem', None, 'lon', 'lat'), may hold values from -6 to 6
- control_mid: bfloat16 [128, 16, 128, 256], P('mem', None, 'lon', 'lat'), may hold values from -6 to 6
- control_coarse: bfloat16 [128, 16, 64, 128], P('mem', None, 'lon', 'lat'), may hold values from -6 to 6
- vertical: bfloat16 [3, 16, 16], replicated, may hold values from 0 to 0.25
- mid_picks: int32 [384], replicated, may hold values from 0 to 1
- coarse_picks: int32 [192], replicated, may hold values from 0 to 3
- band_radii: int32 [3], replicated, may hold values from 4 to 8
Outputs:
- increment: float32 [8, 512, 512], P('lon', 'mem', 'lat')
The draws below stay inside these ranges and needn't reach their ends.
Inputs may be any that keep to these rules, and one draw needn't show every extreme that they name: `mid_picks`: entry i of the first 256 entries picks fine row 2 i + entry for middle-band row i; entry j of the rest picks fine column 2 j + entry for middle-band column j. `coarse_picks`: entry i of the first 128 entries picks fine row 4 i + entry for coarse-band row i; entry j of the rest picks fine column 4 j + entry for coarse-band column j. `band_radii`: radius of each band's horizontal taper, in that band's cells.
All inputs are finite; a program needn't handle non-finite values.
Results may differ from the reference program's by a relative error of at most 0.0062.
Values may be sent and summed in bfloat16 or wider, within the bound.
No kernel may reach another device: no remote copies, remote signals or barrier semaphores. Data moves between devices by JAX's collectives and lax.ppermute only.
A program may use at most 32 MiB of HBM per device.

```python
import math
import jax
import jax.numpy as jnp
from jax import lax

LEV = 16
REACH = 8
COLS_DEV = 32
MEMBERS = 128
NLAT = 512
NLON = 256
N_LON = 8


def set_ends(array, rng, low, top_value):
    shape = array.shape
    place = [jax.random.randint(jax.random.fold_in(rng, axis), (), 0, shape[axis]) for axis in range(len(shape))]
    array = array.at[tuple(place)].set(low)
    longest = shape.index(max(shape))
    place[longest] = (place[longest] + 1) % shape[longest]
    return array.at[tuple(place)].set(top_value)


def raised(entries, own_key, source, target, shards_of, factor):
    owner, partner = [(jnp.arange(entries.shape[dim]) // (entries.shape[dim] // shards_of)).reshape([-1 if axis == dim else 1 for axis in range(entries.ndim)]) for dim in (source, target)]
    chosen = jax.random.permutation(own_key, shards_of)[partner]
    strong = (owner == chosen) | (owner == (partner + shards_of // 2) % shards_of)
    return jnp.where(strong, factor * entries, entries)


def block_levels(own_key, extent, shards, smallest, high):
    factor_of = 1.0
    for position, blocks in shards:
        steps = jax.random.uniform(jax.random.fold_in(jax.random.fold_in(own_key, 6), position), (blocks,), jnp.float32, smallest / len(shards), high / len(shards))
        factor_of = factor_of * jnp.repeat(jnp.exp(steps), extent[position] // blocks).reshape((-1,) + (1,) * (len(extent) - 1 - position))
    return factor_of


def gaussian(stream_key, dims, scale, bound, split=(), kind=jnp.bfloat16):
    values = jax.random.normal(stream_key, dims, jnp.float32) * scale
    if len(split) > 0:
        values = block_levels(stream_key, dims, split, -0.22, 0.18) * values
    return jnp.clip(values, min=-bound, max=bound).astype(kind)


def bell_draw_with(stream_key, extent, scale, bound, shards, heavy, kind=jnp.bfloat16):
    drawn = scale * jax.random.normal(stream_key, extent, jnp.float32)
    if shards:
        drawn = drawn * block_levels(stream_key, extent, shards, -0.22, 0.18)
    return jnp.clip(raised(drawn, jax.random.fold_in(stream_key, 3), *heavy), -bound, bound).astype(kind)


def setup_inputs(seed: int = 0) -> dict:
    splits = jax.random.split(jax.random.key(seed), 9)
    return {
        "members": bell_draw_with(splits[0], (MEMBERS, LEV, NLON, NLAT), 1.0, 16.0, ((0, 64), (2, 8), (3, 2)), (0, 2, 64, 4.0)),
        "control_fine": gaussian(splits[1], (MEMBERS, LEV, NLON, NLAT), 1.0, 6.0, ((0, 64), (2, 8), (3, 2))),
        "control_mid": gaussian(splits[2], (MEMBERS, LEV, NLON // 2, NLAT // 2), 1.0, 6.0, ((0, 64), (2, 8), (3, 2))),
        "control_coarse": gaussian(splits[3], (MEMBERS, LEV, NLON // 4, NLAT // 4), 1.0, 6.0, ((0, 64), (2, 8), (3, 2))),
        "vertical": jnp.clip(jax.random.uniform(splits[4], (3, LEV, LEV), jnp.float32, 0.0, 0.25), 0.0, 0.25).astype(jnp.bfloat16),
        "mid_picks": set_ends(jax.random.randint(splits[5], (NLAT // 2 + NLON // 2,), 0, 2), jax.random.fold_in(splits[5], 1), 0, 1).astype(jnp.int32),
        "coarse_picks": set_ends(jax.random.randint(splits[6], (NLAT // 4 + NLON // 4,), 0, 4), jax.random.fold_in(splits[6], 1), 0, 3).astype(jnp.int32),
        "band_radii": jax.random.randint(splits[7], (3,), 4, 9).astype(jnp.int32),
    }


band_factors = (1, 2, 4)

def tap_weights(radius):
    offsets = jnp.arange(-REACH, REACH + 1).astype(jnp.float32)
    reach_now = radius.astype(jnp.float32)
    spread = 0.5 * reach_now
    unnormed = jnp.where(jnp.abs(offsets) <= reach_now, jnp.exp(-0.5 * jnp.square(offsets / spread)), jnp.float32(0.0))
    return (unnormed / jnp.sum(unnormed)).astype(jnp.bfloat16)

def localize(control, vertical_band, weights):
    mixed = jnp.einsum('kl,lcr->kcr', vertical_band.astype(jnp.float32), control.astype(jnp.float32), precision=lax.Precision.HIGHEST).astype(jnp.bfloat16)
    length = mixed.shape[2]
    padded = jnp.pad(mixed, ((0, 0), (0, 0), (REACH, REACH))).astype(jnp.float32)
    weight_wide = weights.astype(jnp.float32)
    across = jnp.zeros(mixed.shape, jnp.float32)
    for offset in range(2 * REACH + 1):
        across = across + weight_wide[offset] * padded[:, :, offset:offset + length]
    across = lax.optimization_barrier(across.astype(jnp.bfloat16)).astype(jnp.float32)
    width_cols = across.shape[1]
    wrapped = jnp.concatenate([across[:, width_cols - REACH:, :], across, across[:, :REACH, :]], axis=1)
    result = jnp.zeros(across.shape, jnp.float32)
    for offset in range(2 * REACH + 1):
        result = result + weight_wide[offset] * wrapped[:, offset:offset + width_cols, :]
    return result

def restrict(member, chosen, factor, row_total):
    band_rows = row_total // factor
    band_cols = chosen.shape[0] - band_rows
    row_pick = factor * jnp.arange(band_rows, dtype=jnp.int32) + chosen[:band_rows].astype(jnp.int32)
    col_pick = factor * jnp.arange(band_cols, dtype=jnp.int32) + chosen[band_rows:].astype(jnp.int32)
    return member[:, col_pick, :][:, :, row_pick]

def prolong(values, factor):
    return jnp.repeat(jnp.repeat(values, factor, axis=1), factor, axis=2)

def reference(members, control_fine, control_mid, control_coarse, vertical, mid_picks, coarse_picks, band_radii):
    member_total = members.shape[0]
    row_total = members.shape[3]
    chosen_all = (None, mid_picks, coarse_picks)
    weight_sets = [tap_weights(band_radii[band_index]) for band_index in range(3)]

    def add_member(accumulated, sliced):
        member = sliced[0]
        for band_index in range(3):
            factor = band_factors[band_index]
            filtered = localize(sliced[band_index + 1], vertical[band_index], weight_sets[band_index])
            if factor == 1:
                restricted = member
            else:
                restricted = restrict(member, chosen_all[band_index], factor, row_total)
            product = restricted.astype(jnp.float32) * filtered
            accumulated = accumulated + prolong(product, factor)
        return (accumulated, None)
    start = jnp.zeros((LEV, NLON, NLAT), jnp.float32)
    accumulated, unused = lax.scan(add_member, start, (members, control_fine, control_mid, control_coarse))
    field = accumulated / math.sqrt(member_total - 1)
    blocks = field.reshape(LEV, N_LON, COLS_DEV, NLAT).transpose(1, 0, 2, 3)
    return blocks.reshape(N_LON, LEV * COLS_DEV, NLAT)
```

```python
import functools
import math

import jax
import jax.numpy as jnp
from jax import lax
from jax.experimental import pallas as pl
from jax.experimental.pallas import tpu as pltpu
from jax.sharding import PartitionSpec as P

REACH = 8
LEV = 16
FACTORS = (1, 2, 4)
B16 = jnp.bfloat16
F32 = jnp.float32


def iota(shape, dim):
    return lax.broadcasted_iota(jnp.int32, shape, dim)


def dot(a, b, ca=1, cb=0):
    return lax.dot_general(a, b, (((ca,), (cb,)), ((), ())), preferred_element_type=F32)


def bell(offset, radius):
    wide = offset.astype(F32)
    reach_now = jnp.broadcast_to(radius.astype(F32), wide.shape)
    raw = jnp.exp(-0.5 * jnp.square(wide / (0.5 * reach_now)))
    return jnp.where(jnp.abs(wide) <= reach_now, raw, 0.0)


def bell_sum(radius):
    lanes = iota((8, 128), 1)
    raw = jnp.where(lanes <= 2 * REACH, bell(lanes - REACH, radius), 0.0)
    return jnp.sum(raw, axis=1, keepdims=True)[0:1]


def taps(offset, radius, total):
    return (bell(offset, radius) / total).astype(B16)


def edge_kernel(sizes, fine, mid, coarse, out):
    low_half = lax.axis_index("lat") == 0
    start = 0
    for ref, (cells, rows) in zip((fine, mid, coarse), sizes):
        base = jnp.where(low_half, rows - REACH, 0)
        pick = (iota((REACH, rows), 1) == iota((REACH, rows), 0) + base).astype(B16)
        out[:, start : start + cells] = dot(pick, ref[...], 1, 1).astype(B16)
        start += cells


def prep_kernel(
    sizes,
    radii,
    members,
    vertical,
    mid_picks,
    coarse_picks,
    row0,
    row1,
    row2,
    rim,
    own0,
    own1,
    own2,
    side0,
    side1,
    side2,
    res1,
    res2,
    spare,
):
    lat = lax.axis_index("lat")
    lon = lax.axis_index("lon")
    cols = sizes[0][0] // members.shape[0] * 32
    bands = zip(FACTORS, sizes, (row0, row1, row2), (own0, own1, own2), (side0, side1, side2))
    for band, (factor, (cells, rows), row_ref, own_ref, side_ref) in enumerate(bands):
        radius = radii[band]
        total = bell_sum(radius)
        width = cols // factor
        row_ref[...] = taps(iota((rows, rows), 0) - iota((rows, rows), 1), radius, total)
        base = jnp.where(lat == 0, rows, -REACH)
        shape = (REACH, rows)
        rim[band, :, :rows] = taps(iota(shape, 0) + base - iota(shape, 1), radius, total)
        for ref, span in ((own_ref, width), (side_ref, REACH)):
            lanes = LEV * span
            shape = (cols, lanes)
            place = iota(shape, 1) % span
            target = iota(shape, 0) // factor
            level = (iota((LEV, lanes), 0) == iota((LEV, lanes), 1) // span).astype(B16)
            spread = dot(vertical[band], level)
            if span == width and ref is own_ref:
                parts = ((0, taps(place - target, radius, total)),)
            else:
                parts = (
                    (0, taps(place - REACH - target, radius, total)),
                    (lanes, taps(place + width - target, radius, total)),
                )
            for at, pattern in parts:
                pattern = pattern.astype(F32)
                for k in range(LEV):
                    block = (spread[k : k + 1] * pattern).astype(B16)
                    ref[k * cols : (k + 1) * cols, at : at + lanes] = block
    full_rows = sizes[0][1]
    block = 8 * cols
    for factor, picks, out in ((2, mid_picks, res1), (4, coarse_picks, res2)):
        n = picks.shape[1]
        rows = full_rows // factor
        width = cols // factor
        values = jnp.broadcast_to(picks[...].astype(F32), (8, n)).astype(B16)
        shape = (n, full_rows)
        hot = (iota(shape, 0) == lat * rows + iota(shape, 1) // factor).astype(B16)
        chosen = dot(values, hot)[0:1]
        shape = (full_rows, full_rows)
        wanted = (factor * (iota((1, full_rows), 1) // factor)).astype(F32) + chosen
        row_pick = (iota(shape, 0).astype(F32) == wanted).astype(B16)
        shape = (cols, n)
        hot = (iota(shape, 1) == 2 * rows + lon * width + iota(shape, 0) // factor).astype(B16)
        chosen = dot(hot, values, 1, 1)[:, 0:1]
        wanted = (factor * (iota((cols, 1), 0) // factor)).astype(F32) + chosen
        lanes = iota((cols, block), 1).astype(F32)
        for k in range(8):
            spare[k * cols : (k + 1) * cols] = (lanes == wanted + F32(k * cols)).astype(B16)
        col_pick = spare[...]
        for part in range(members.shape[0] // block):
            at = slice(part * block, (part + 1) * block)
            by_rows = dot(members[at], row_pick).astype(B16)
            out[at] = dot(col_pick, by_rows).astype(B16)


def rows_kernel(sizes, fine, mid, coarse, rim_in, row0, row1, row2, rim, out0, out1, out2, right, left):
    start = 0
    lane = 0
    bands = zip(FACTORS, sizes, (fine, mid, coarse), (row0, row1, row2), (out0, out1, out2))
    for band, (factor, (cells, rows), ref, row_ref, out) in enumerate(bands):
        width = 32 // factor
        matrix = row_ref[...]
        edge = rim[band, :, :rows]
        chunk = 128
        groups = chunk // width
        for part in range(cells // chunk):
            at = slice(part * chunk, (part + 1) * chunk)
            arrived = rim_in[:, start + part * chunk : start + (part + 1) * chunk]
            across = dot(ref[at], matrix) + dot(arrived, edge, 0, 0)
            out[at] = across.astype(B16)
            cut = across.reshape(groups, width, rows)
            to = slice(part * groups * REACH, (part + 1) * groups * REACH)
            right[to, lane : lane + rows] = cut[:, width - REACH :].reshape(-1, rows).astype(B16)
            left[to, lane : lane + rows] = cut[:, :REACH].reshape(-1, rows).astype(B16)
        start += cells
        lane += rows


def widen(values, factor):
    if factor == 1:
        return values
    rows = values.shape[1]
    shape = (rows, rows * factor)
    return dot(values, (iota(shape, 0) == iota(shape, 1) // factor).astype(B16)).astype(B16)


def own_kernel(sizes, acr0, acr1, acr2, own0, own1, own2, members, res1, res2, out):
    first = True
    bands = zip(FACTORS, sizes, (acr0, acr1, acr2), (own0, own1, own2), (members, res1, res2))
    for factor, (cells, rows), acr, own, res in bands:
        half = cells // 2
        size = res.shape[0] // 2
        for m in range(2):
            local = dot(own[...], widen(acr[m * half : (m + 1) * half], factor))
            product = local * res[m * size : (m + 1) * size].astype(F32)
            out[...] = product if first else out[...] + product
            first = False


def side_kernel(sizes, from_left, from_right, side0, side1, side2, members, res1, res2, partial, out, total):
    lane = 0
    total[...] = partial[...]
    bands = zip(FACTORS, sizes, (side0, side1, side2), (members, res1, res2))
    for factor, (cells, rows), side, res in bands:
        half = from_left.shape[0] // 2
        size = res.shape[0] // 2
        for m in range(2):
            at = slice(m * half, (m + 1) * half)
            both = jnp.concatenate(
                [from_left[at, lane : lane + rows], from_right[at, lane : lane + rows]], axis=0
            )
            local = dot(side[...], widen(both, factor))
            total[...] += local * res[m * size : (m + 1) * size].astype(F32)
        lane += rows
    out[...] = total[...].astype(B16)


VMEM = pl.BlockSpec(memory_space=pltpu.VMEM)
SMEM = pl.BlockSpec(memory_space=pltpu.SMEM)


def call(kernel, outs, in_specs, scratch=(), flops=0, limit=24):
    shapes = [jax.ShapeDtypeStruct(shape, kind) for shape, kind in outs]
    many = len(shapes) > 1
    return pl.pallas_call(
        kernel,
        out_shape=shapes if many else shapes[0],
        in_specs=in_specs,
        out_specs=[VMEM] * len(shapes) if many else VMEM,
        scratch_shapes=scratch,
        compiler_params=pltpu.CompilerParams(vmem_limit_bytes=limit << 20),
        cost_estimate=pl.CostEstimate(flops=flops, bytes_accessed=1 << 20, transcendentals=0),
    )


def on_device(
    members,
    control_fine,
    control_mid,
    control_coarse,
    vertical,
    mid_picks,
    coarse_picks,
    band_radii,
):
    devices = lax.axis_size("mem")
    member_total = members.shape[0] * devices
    held = members.shape[0] * LEV
    members = members.reshape(held * members.shape[2], members.shape[3])
    controls = [c.reshape(held * c.shape[2], c.shape[3]) for c in (control_fine, control_mid, control_coarse)]
    sizes = tuple(c.shape for c in controls)
    all_cells = sum(cells for cells, _ in sizes)
    all_rows = sum(rows for _, rows in sizes)
    fine_cells, fine_rows = sizes[0]
    out_cells = fine_cells // 2

    edge = call(
        functools.partial(edge_kernel, sizes), [((REACH, all_cells), B16)], [VMEM] * 3, flops=10**7
    )(*controls)
    with jax.named_scope("lat_swap"):
        arrived = lax.ppermute(edge, "lat", [(0, 1), (1, 0)])

    outs = [((rows, rows), B16) for _, rows in sizes]
    outs += [((3, REACH, fine_rows), B16)]
    outs += [((out_cells, cells // 2), B16) for cells, _ in sizes]
    outs += [((out_cells, 2 * LEV * REACH), B16)] * 3
    outs += [((fine_cells, fine_rows), B16)] * 2
    prep = call(
        functools.partial(prep_kernel, sizes),
        outs,
        [SMEM] + [VMEM] * 4,
        [pltpu.VMEM((256, 256), B16)],
        flops=10**9,
    )(band_radii, members, vertical, mid_picks[None], coarse_picks[None])
    rows = prep[0:3]
    rim = prep[3]
    own = prep[4:7]
    side = prep[7:10]
    res = prep[10:12]

    filtered = call(
        functools.partial(rows_kernel, sizes),
        [(s, B16) for s in sizes] + [((held * REACH, all_rows), B16)] * 2,
        [VMEM] * 8,
        flops=2 * 10**8,
    )(*controls, arrived, *rows, rim)
    across = filtered[0:3]
    count = lax.axis_size("lon")
    with jax.named_scope("lon_right"):
        from_left = lax.ppermute(filtered[3], "lon", [(i, (i + 1) % count) for i in range(count)])
    with jax.named_scope("lon_left"):
        from_right = lax.ppermute(filtered[4], "lon", [((i + 1) % count, i) for i in range(count)])

    partial = call(
        functools.partial(own_kernel, sizes),
        [((out_cells, fine_rows), F32)],
        [VMEM] * 9,
        flops=10**9,
    )(*across, *own, members, *res)
    field = call(
        functools.partial(side_kernel, sizes),
        [((out_cells, fine_rows), B16)],
        [VMEM] * 9,
        [pltpu.VMEM((out_cells, fine_rows), F32)],
        flops=10**9,
    )(from_left, from_right, *side, members, *res, partial)

    blocks = field.reshape(devices, out_cells // devices, fine_rows)
    blocks = lax.all_to_all(blocks, "mem", split_axis=0, concat_axis=0, tiled=True)
    increment = blocks.astype(F32).sum(axis=0) / math.sqrt(member_total - 1)
    return increment[None, :, :]


def solution(mesh):
    placed = (
        P("mem", None, "lon", "lat"),
        P("mem", None, "lon", "lat"),
        P("mem", None, "lon", "lat"),
        P("mem", None, "lon", "lat"),
        P(),
        P(),
        P(),
        P(),
    )
    return jax.shard_map(
        on_device, mesh=mesh, in_specs=placed, out_specs=P("lon", "mem", "lat"), check_vma=False
    )
```

```python
import functools
import math

import jax
import jax.numpy as jnp
from jax import lax
from jax.experimental import pallas as pl
from jax.experimental.pallas import tpu as pltpu
from jax.sharding import PartitionSpec as P

REACH = 8
LEV = 16
FACTORS = (1, 2, 4)
B16 = jnp.bfloat16
F32 = jnp.float32


def iota(shape, dim):
    return lax.broadcasted_iota(jnp.int32, shape, dim)


def dot(a, b, ca=1, cb=0):
    return lax.dot_general(a, b, (((ca,), (cb,)), ((), ())), preferred_element_type=F32)


def bell(offset, radius):
    wide = offset.astype(F32)
    reach_now = jnp.broadcast_to(radius.astype(F32), wide.shape)
    raw = jnp.exp(-0.5 * jnp.square(wide / (0.5 * reach_now)))
    return jnp.where(jnp.abs(wide) <= reach_now, raw, 0.0)


def bell_sum(radius):
    lanes = iota((8, 128), 1)
    raw = jnp.where(lanes <= 2 * REACH, bell(lanes - REACH, radius), 0.0)
    return jnp.sum(raw, axis=1, keepdims=True)[0:1]


def taps(offset, radius, total):
    return (bell(offset, radius) / total).astype(B16)


def edge_kernel(sizes, fine, mid, coarse, out, buf0, buf1, buf2, sems):
    low_half = lax.axis_index("lat") == 0
    copies = []
    for band, (ref, buf) in enumerate(zip((fine, mid, coarse), (buf0, buf1, buf2))):
        width = buf.shape[1]
        if width < ref.shape[1]:
            first = pl.multiple_of(jnp.where(low_half, ref.shape[1] - width, 0), width)
            ref = ref.at[:, pl.ds(first, width)]
        copies.append(pltpu.make_async_copy(ref, buf, sems.at[band]))
    for copy in copies:
        copy.start()
    start = 0
    for copy, buf in zip(copies, (buf0, buf1, buf2)):
        cells, width = buf.shape
        base = jnp.where(low_half, width - REACH, 0)
        pick = (iota((REACH, width), 1) == iota((REACH, width), 0) + base).astype(B16)
        copy.wait()
        out[:, start : start + cells] = dot(pick, buf[...], 1, 1).astype(B16)
        start += cells


def prep_kernel(
    sizes,
    radii,
    members,
    vertical,
    mid_picks,
    coarse_picks,
    fine,
    mid,
    coarse,
    xr0,
    xr1,
    xr2,
    rim,
    own0,
    own1,
    own2,
    side0,
    side1,
    side2,
    res1,
    res2,
    spare,
    buf0,
    buf1,
    buf2,
    sems,
):
    lat = lax.axis_index("lat")
    lon = lax.axis_index("lon")
    cols = 32
    copies = []
    for band, (ref, buf) in enumerate(zip((fine, mid, coarse), (buf0, buf1, buf2))):
        copies.append(pltpu.make_async_copy(ref, buf, sems.at[band]))
        copies[band].start()
    alongs = []
    refs = zip((own0, own1, own2), (side0, side1, side2))
    for band, (factor, (cells, rows), (own_ref, side_ref)) in enumerate(zip(FACTORS, sizes, refs)):
        radius = radii[band]
        total = bell_sum(radius)
        width = cols // factor
        alongs.append(taps(iota((rows, rows), 0) - iota((rows, rows), 1), radius, total))
        base = jnp.where(lat == 0, rows, -REACH)
        shape = (REACH, rows)
        rim[band, :, :rows] = taps(iota(shape, 0) + base - iota(shape, 1), radius, total)
        reach_cols = factor * REACH
        parts = (
            (own_ref, 0, width, cols, 0, 0),
            (side_ref, 0, REACH, reach_cols, 0, -REACH),
            (side_ref, LEV * REACH, REACH, reach_cols, cols - reach_cols, width),
        )
        for to, at, span, count, first, shift in parts:
            lanes = LEV * span
            place = iota((count, lanes), 1) % span + shift
            target = (iota((count, lanes), 0) + first) // factor
            pattern = taps(place - target, radius, total).astype(F32)
            level = (iota((LEV, lanes), 0) == iota((LEV, lanes), 1) // span).astype(B16)
            spread = dot(vertical[band], level)
            for k in range(LEV):
                to[k * count : (k + 1) * count, at : at + lanes] = (spread[k : k + 1] * pattern).astype(B16)
    for copy, buf, along, xr in zip(copies, (buf0, buf1, buf2), alongs, (xr0, xr1, xr2)):
        copy.wait()
        xr[...] = dot(buf[...], along)
    full_rows = sizes[0][1]
    block = 8 * cols
    for factor, picks, out in ((2, mid_picks, res1), (4, coarse_picks, res2)):
        n = picks.shape[1]
        rows = full_rows // factor
        width = cols // factor
        values = jnp.broadcast_to(picks[...].astype(F32), (8, n)).astype(B16)
        shape = (n, full_rows)
        hot = (iota(shape, 0) == lat * rows + iota(shape, 1) // factor).astype(B16)
        chosen = dot(values, hot)[0:1]
        shape = (full_rows, full_rows)
        wanted = (factor * (iota((1, full_rows), 1) // factor)).astype(F32) + chosen
        row_pick = (iota(shape, 0).astype(F32) == wanted).astype(B16)
        shape = (cols, n)
        hot = (iota(shape, 1) == 2 * rows + lon * width + iota(shape, 0) // factor).astype(B16)
        chosen = dot(hot, values, 1, 1)[:, 0:1]
        wanted = (factor * (iota((cols, 1), 0) // factor)).astype(F32) + chosen
        lanes = iota((cols, block), 1).astype(F32)
        for k in range(8):
            spare[k * cols : (k + 1) * cols] = (lanes == wanted + F32(k * cols)).astype(B16)
        col_pick = spare[...]
        for part in range(members.shape[0] // block):
            at = slice(part * block, (part + 1) * block)
            by_rows = dot(members[at], row_pick).astype(B16)
            out[at] = dot(col_pick, by_rows).astype(B16)


def rows_kernel(sizes, rim_in, xr0, xr1, xr2, rim, out0, out1, out2, odd, even):
    sends_left_first = lax.axis_index("lon") % 2 == 0
    start = 0
    lane = 0
    bands = zip(FACTORS, sizes, (xr0, xr1, xr2), (out0, out1, out2))
    for band, (factor, (cells, rows), xr, out) in enumerate(bands):
        width = 32 // factor
        edge = rim[band, :, :rows]
        chunk = 128
        groups = chunk // width
        for part in range(cells // chunk):
            at = slice(part * chunk, (part + 1) * chunk)
            arrived = rim_in[:, start + part * chunk : start + (part + 1) * chunk]
            across = xr[at] + dot(arrived, edge, 0, 0)
            out[at] = across.astype(B16)
            cut = across.reshape(groups, width, rows)
            right = cut[:, width - REACH :].reshape(-1, rows)
            left = cut[:, :REACH].reshape(-1, rows)
            to = slice(part * groups * REACH, (part + 1) * groups * REACH)
            odd[to, lane : lane + rows] = jnp.where(sends_left_first, left, right).astype(B16)
            even[to, lane : lane + rows] = jnp.where(sends_left_first, right, left).astype(B16)
        start += cells
        lane += rows


def widen(values, factor):
    if factor == 1:
        return values
    rows = values.shape[1]
    shape = (rows, rows * factor)
    return dot(values, (iota(shape, 0) == iota(shape, 1) // factor).astype(B16)).astype(B16)


def own_kernel(sizes, acr0, acr1, acr2, own0, own1, own2, members, res1, res2, out):
    first = True
    bands = zip(FACTORS, sizes, (acr0, acr1, acr2), (own0, own1, own2), (members, res1, res2))
    for factor, (cells, rows), acr, own, res in bands:
        half = cells // 2
        size = res.shape[0] // 2
        for m in range(2):
            local = dot(own[...], widen(acr[m * half : (m + 1) * half], factor))
            product = local * res[m * size : (m + 1) * size].astype(F32)
            out[...] = product if first else out[...] + product
            first = False


def side_kernel(sizes, odd, even, side0, side1, side2, members, res1, res2, partial, out, total):
    left_is_odd = lax.axis_index("lon") % 2 == 0
    total[...] = partial[...].reshape(total.shape)
    half = odd.shape[0] // 2
    size = members.shape[0] // 2
    cols = total.shape[1]
    lane = 0
    bands = zip(FACTORS, sizes, (side0, side1, side2), (members, res1, res2))
    for factor, (cells, rows), side, res in bands:
        count = factor * REACH
        for m in range(2):
            at = slice(m * half, (m + 1) * half)
            one = odd[at, lane : lane + rows]
            two = even[at, lane : lane + rows]
            left = jnp.where(left_is_odd, one, two)
            right = jnp.where(left_is_odd, two, one)
            weight = res[m * size : (m + 1) * size].reshape(total.shape)
            if count == cols:
                local = dot(side[...], widen(jnp.concatenate([left, right], axis=0), factor))
                total[...] += local.reshape(total.shape) * weight.astype(F32)
                continue
            for begin, first, came in ((0, 0, left), (half, cols - count, right)):
                local = dot(side[:, begin : begin + half], widen(came, factor))
                where = slice(first, first + count)
                local = local.reshape(LEV, count, -1)
                total[:, where] += local * weight[:, where].astype(F32)
        lane += rows
    out[...] = total[...].reshape(out.shape).astype(B16)


VMEM = pl.BlockSpec(memory_space=pltpu.VMEM)
SMEM = pl.BlockSpec(memory_space=pltpu.SMEM)
HBM = pl.BlockSpec(memory_space=pltpu.HBM)


def call(kernel, outs, in_specs, scratch=(), flops=0, limit=24):
    shapes = [jax.ShapeDtypeStruct(shape, kind) for shape, kind in outs]
    many = len(shapes) > 1
    return pl.pallas_call(
        kernel,
        out_shape=shapes if many else shapes[0],
        in_specs=in_specs,
        out_specs=[VMEM] * len(shapes) if many else VMEM,
        scratch_shapes=scratch,
        compiler_params=pltpu.CompilerParams(vmem_limit_bytes=limit << 20),
        cost_estimate=pl.CostEstimate(flops=flops, bytes_accessed=1 << 20, transcendentals=0),
    )


def on_device(
    members,
    control_fine,
    control_mid,
    control_coarse,
    vertical,
    mid_picks,
    coarse_picks,
    band_radii,
):
    devices = lax.axis_size("mem")
    member_total = members.shape[0] * devices
    held = members.shape[0] * LEV
    members = members.reshape(held * members.shape[2], members.shape[3])
    controls = [c.reshape(held * c.shape[2], c.shape[3]) for c in (control_fine, control_mid, control_coarse)]
    sizes = tuple(c.shape for c in controls)
    all_cells = sum(cells for cells, _ in sizes)
    all_rows = sum(rows for _, rows in sizes)
    fine_cells, fine_rows = sizes[0]
    out_cells = fine_cells // 2

    edge = call(
        functools.partial(edge_kernel, sizes),
        [((REACH, all_cells), B16)],
        [HBM] * 3,
        [pltpu.VMEM((cells, min(rows, 128)), B16) for cells, rows in sizes] + [pltpu.SemaphoreType.DMA((3,))],
        flops=10**7,
    )(*[pltpu.with_memory_space_constraint(c, pltpu.HBM) for c in controls])
    with jax.named_scope("lat_swap"):
        arrived = lax.ppermute(edge, "lat", [(0, 1), (1, 0)])

    outs = [(s, F32) for s in sizes]
    outs += [((3, REACH, fine_rows), B16)]
    outs += [((out_cells, cells // 2), B16) for cells, _ in sizes]
    outs += [((LEV * factor * REACH, 2 * LEV * REACH), B16) for factor in FACTORS]
    outs += [((fine_cells, fine_rows), B16)] * 2
    prep = call(
        functools.partial(prep_kernel, sizes),
        outs,
        [SMEM] + [VMEM] * 4 + [HBM] * 3,
        [pltpu.VMEM((256, 256), B16)] + [pltpu.VMEM(s, B16) for s in sizes] + [pltpu.SemaphoreType.DMA((3,))],
        flops=10**9,
    )(band_radii, members, vertical, mid_picks[None], coarse_picks[None], *controls)
    filtered = prep[0:3]
    rim = prep[3]
    own = prep[4:7]
    side = prep[7:10]
    res = prep[10:12]

    filtered = call(
        functools.partial(rows_kernel, sizes),
        [(s, B16) for s in sizes] + [((held * REACH, all_rows), B16)] * 2,
        [VMEM] * 5,
        flops=2 * 10**8,
    )(arrived, *filtered, rim)
    across = filtered[0:3]
    count = lax.axis_size("lon")
    pairs = [(i, (i + 1) % count) for i in range(1, count, 2)]
    with jax.named_scope("lon_odd"):
        odd = lax.ppermute(filtered[3], "lon", pairs + [(j, i) for i, j in pairs])
    pairs = [(i, i + 1) for i in range(0, count, 2)]
    with jax.named_scope("lon_even"):
        even = lax.ppermute(filtered[4], "lon", pairs + [(j, i) for i, j in pairs])

    partial = call(
        functools.partial(own_kernel, sizes),
        [((out_cells, fine_rows), F32)],
        [VMEM] * 9,
        flops=10**9,
    )(*across, *own, members, *res)
    field = call(
        functools.partial(side_kernel, sizes),
        [((out_cells, fine_rows), B16)],
        [VMEM] * 9,
        [pltpu.VMEM((LEV, out_cells // LEV, fine_rows), F32)],
        flops=10**9,
    )(odd, even, *side, members, *res, partial)

    blocks = field.reshape(devices, out_cells // devices, fine_rows)
    blocks = lax.all_to_all(blocks, "mem", split_axis=0, concat_axis=0, tiled=True)
    increment = blocks.astype(F32).sum(axis=0) / math.sqrt(member_total - 1)
    return increment[None, :, :]


def solution(mesh):
    placed = (
        P("mem", None, "lon", "lat"),
        P("mem", None, "lon", "lat"),
        P("mem", None, "lon", "lat"),
        P("mem", None, "lon", "lat"),
        P(),
        P(),
        P(),
        P(),
    )
    return jax.shard_map(
        on_device, mesh=mesh, in_specs=placed, out_specs=P("lon", "mem", "lat"), check_vma=False
    )
```

```python
import functools
import math

import jax
import jax.numpy as jnp
from jax import lax
from jax.experimental import pallas as pl
from jax.experimental.pallas import tpu as pltpu
from jax.sharding import PartitionSpec as P


REACH = 8
LEV = 16
FACTORS = (1, 2, 4)
B16 = jnp.bfloat16
F32 = jnp.float32


def iota(shape, dim):
    return lax.broadcasted_iota(jnp.int32, shape, dim)


def dot(a, b, ca=1, cb=0):
    return lax.dot_general(a, b, (((ca,), (cb,)), ((), ())), preferred_element_type=F32)


def bell(offset, radius):
    wide = offset.astype(F32)
    reach_now = jnp.broadcast_to(radius.astype(F32), wide.shape)
    raw = jnp.exp(-0.5 * jnp.square(wide / (0.5 * reach_now)))
    return jnp.where(jnp.abs(wide) <= reach_now, raw, 0.0)


def bell_sum(radius):
    lanes = iota((8, 128), 1)
    raw = jnp.where(lanes <= 2 * REACH, bell(lanes - REACH, radius), 0.0)
    return jnp.sum(raw, axis=1, keepdims=True)[0:1]


def taps(offset, radius, total):
    return (bell(offset, radius) / total).astype(B16)


def edge_kernel(fine, mid, coarse, out, odd, even, buf0, buf1, buf2, buf3, sems):
    low_half = lax.axis_index("lat") == 0
    left_is_odd = lax.axis_index("lon") % 2 == 0
    copies = []

    def begin(source, to):
        copies.append(pltpu.make_async_copy(source, to, sems.at[len(copies)]))
        copies[-1].start()

    held = fine.shape[0]
    first = pl.multiple_of(jnp.where(low_half, fine.shape[2] - 128, 0), 128)
    for ref, buf, lanes in ((coarse, buf2, None), (mid, buf1, None), (fine, buf0, first)):
        for group in range(ref.shape[1] // REACH):
            source = ref.at[:, group * REACH : (group + 1) * REACH]
            if lanes is not None:
                source = ref.at[:, group * REACH : (group + 1) * REACH, pl.ds(lanes, 128)]
            begin(source, buf.at[group])
    for_rows = len(copies)
    begin(coarse, buf3)
    for to, goes_left in ((odd, left_is_odd), (even, jnp.logical_not(left_is_odd))):
        at = 0
        for ref in (fine, mid):
            column = pl.multiple_of(jnp.where(goes_left, 0, ref.shape[1] - REACH), REACH)
            for lane in range(0, ref.shape[2], 128):
                begin(ref.at[:, pl.ds(column, REACH), lane : lane + 128], to.at[at : at + held])
                at += held
    for copy in copies[:for_rows]:
        copy.wait()
    start = 0
    for buf in (buf0, buf1, buf2):
        width = buf.shape[-1]
        base = jnp.where(low_half, width - REACH, 0)
        pick = (iota((REACH, width), 1) == iota((REACH, width), 0) + base).astype(B16)
        cells = buf.shape[0] * held * REACH
        rows = buf[...].astype(F32).reshape(cells, width).astype(B16)
        out[:, start : start + cells] = dot(pick, rows, 1, 1).astype(B16)
        start += cells
    copies[for_rows].wait()
    for to in (odd, even):
        to[3 * held :, :, : buf3.shape[2]] = buf3[...]
    for copy in copies[for_rows + 1 :]:
        copy.wait()


def prep_kernel(
    sizes,
    radii,
    members,
    vertical,
    mid_picks,
    coarse_picks,
    fine,
    mid,
    coarse,
    xr0,
    xr1,
    xr2,
    row0,
    row1,
    row2,
    rim,
    own0,
    own1,
    own2,
    side0,
    side1,
    side2,
    res1,
    res2,
    spare,
    buf0,
    buf1,
    buf2,
    sems,
):
    lat = lax.axis_index("lat")
    lon = lax.axis_index("lon")
    cols = 32
    copies = []
    for band, (ref, buf) in enumerate(zip((fine, mid, coarse), (buf0, buf1, buf2))):
        copies.append(pltpu.make_async_copy(ref, buf, sems.at[band]))
        copies[band].start()
    refs = zip((row0, row1, row2), (own0, own1, own2), (side0, side1, side2))
    for band, (factor, (cells, rows), (row_ref, own_ref, side_ref)) in enumerate(zip(FACTORS, sizes, refs)):
        radius = radii[band]
        total = bell_sum(radius)
        width = cols // factor
        shape = (rows, rows * factor)
        row_ref[...] = taps(iota(shape, 0) - iota(shape, 1) // factor, radius, total)
        base = jnp.where(lat == 0, rows, -REACH)
        shape = (REACH, rows * factor)
        rim[band] = taps(iota(shape, 0) + base - iota(shape, 1) // factor, radius, total)
        reach_cols = factor * REACH
        parts = (
            (own_ref, 0, width, cols, 0, 0),
            (side_ref, 0, REACH, reach_cols, 0, -REACH),
            (side_ref, LEV * REACH, REACH, reach_cols, cols - reach_cols, width),
        )
        for to, at, span, count, first, shift in parts:
            lanes = LEV * span
            place = iota((count, lanes), 1) % span + shift
            target = (iota((count, lanes), 0) + first) // factor
            pattern = taps(place - target, radius, total).astype(F32)
            level = (iota((LEV, lanes), 0) == iota((LEV, lanes), 1) // span).astype(B16)
            spread = dot(vertical[band], level)
            for k in range(LEV):
                to[k * count : (k + 1) * count, at : at + lanes] = (spread[k : k + 1] * pattern).astype(B16)
    for copy, buf, row_ref, xr in zip(copies, (buf0, buf1, buf2), (row0, row1, row2), (xr0, xr1, xr2)):
        copy.wait()
        xr[...] = dot(buf[...], row_ref[...])
    full_rows = sizes[0][1]
    block = 8 * cols
    for factor, picks, out in ((2, mid_picks, res1), (4, coarse_picks, res2)):
        n = picks.shape[1]
        rows = full_rows // factor
        width = cols // factor
        values = jnp.broadcast_to(picks[...].astype(F32), (8, n)).astype(B16)
        shape = (n, full_rows)
        hot = (iota(shape, 0) == lat * rows + iota(shape, 1) // factor).astype(B16)
        chosen = dot(values, hot)[0:1]
        shape = (full_rows, full_rows)
        wanted = (factor * (iota((1, full_rows), 1) // factor)).astype(F32) + chosen
        row_pick = (iota(shape, 0).astype(F32) == wanted).astype(B16)
        shape = (cols, n)
        hot = (iota(shape, 1) == 2 * rows + lon * width + iota(shape, 0) // factor).astype(B16)
        chosen = dot(hot, values, 1, 1)[:, 0:1]
        wanted = (factor * (iota((cols, 1), 0) // factor)).astype(F32) + chosen
        lanes = iota((cols, block), 1).astype(F32)
        for k in range(8):
            spare[k * cols : (k + 1) * cols] = (lanes == wanted + F32(k * cols)).astype(B16)
        col_pick = spare[...]
        for part in range(members.shape[0] // block):
            at = slice(part * block, (part + 1) * block)
            by_rows = dot(members[at], row_pick).astype(B16)
            out[at] = dot(col_pick, by_rows).astype(B16)


def forward_kernel(sizes, rim_in, main, odd, even):
    left_is_odd = lax.axis_index("lon") % 2 == 0
    start = 0
    span = main.shape[0] // 4 * REACH
    even[: main.shape[0]] = main[...]
    for band, (cells, rows) in enumerate(sizes):
        for part in range(0, span, 128):
            left = rim_in[:, start + part : start + part + 128]
            right = rim_in[:, start + cells - span + part : start + cells - span + part + 128]
            at = band * span + part
            odd[:, at : at + 128] = jnp.where(left_is_odd, left, right)
            even[main.shape[0] + at // 128] = jnp.where(left_is_odd, right, left)
        start += cells


def own_kernel(sizes, rim_in, xr0, xr1, xr2, rim, own0, own1, own2, members, res1, res2, out):
    first = True
    start = 0
    held = 2 * LEV
    bands = zip(FACTORS, sizes, (xr0, xr1, xr2), (own0, own1, own2), (members, res1, res2))
    for band, (factor, (cells, rows), xr, own, res) in enumerate(bands):
        width = cells // held
        size = res.shape[0] // 2
        edge = rim[band]
        span = LEV * REACH
        for m in range(2):
            sums = xr[m * cells // 2 : (m + 1) * cells // 2].reshape(LEV, width, -1)
            parts = []
            for group in range(width // REACH):
                at = start + (2 * group + m) * span
                parts.append(dot(rim_in[:, at : at + span], edge, 0, 0).reshape(LEV, REACH, -1))
            sums = sums + (parts[0] if len(parts) == 1 else jnp.concatenate(parts, axis=1))
            across = sums.reshape(LEV * width, -1).astype(B16)
            product = dot(own[...], across) * res[m * size : (m + 1) * size].astype(F32)
            out[...] = product if first else out[...] + product
            first = False
        start += cells


def side_kernel(
    sizes,
    odd,
    odd_rim,
    even,
    even_rim,
    row0,
    row1,
    row2,
    rim,
    side0,
    side1,
    side2,
    members,
    res1,
    res2,
    partial,
    out,
    total,
):
    left_is_odd = lax.axis_index("lon") % 2 == 0
    size = members.shape[0] // 2
    cols = total.shape[1]
    span = 2 * LEV * REACH
    half = span // 2
    tiles = even_rim.shape[0] - 6
    at = 3 * span
    order = []
    bands = zip(FACTORS, sizes, (row0, row1, row2), (side0, side1, side2), (members, res1, res2))
    for band, (factor, (cells, rows), row_ref, side, res) in reversed(list(enumerate(bands))):
        both = [0.0, 0.0]
        for lane in reversed(range(0, rows, 128)):
            wide = min(rows, 128)
            one = odd[at : at + span, :wide]
            two = even[at : at + span, :wide]
            at -= span
            matrix = row_ref[lane : lane + wide]
            both[0] += dot(jnp.where(left_is_odd, one, two), matrix)
            both[1] += dot(jnp.where(left_is_odd, two, one), matrix)
        for m in range(2):
            one = odd_rim[:, band * span + m * half : band * span + (m + 1) * half]
            two = even_rim[tiles + 2 * band + m]
            edges = (jnp.where(left_is_odd, one, two), jnp.where(left_is_odd, two, one))
            left, right = [
                (main[m * half : (m + 1) * half] + dot(edge, rim[band], 0, 0)).astype(B16)
                for main, edge in zip(both, edges)
            ]
            order.append((factor, side, res, m, left, right))
    order = order[:1] + order[2:] + order[1:2]
    shape = total.shape
    for step, (factor, side, res, m, left, right) in enumerate(order):
        weight = res[m * size : (m + 1) * size]
        count = factor * REACH
        if count == cols:
            product = dot(side[...], jnp.concatenate([left, right], axis=0)) * weight.astype(F32)
            if step == 0:
                total[...] = (partial[...] + product).reshape(shape)
            else:
                out[...] = (total[...].reshape(out.shape) + product).astype(B16)
            continue
        weight = weight.reshape(shape)
        for begin, first, came in ((0, 0, left), (half, cols - count, right)):
            local = dot(side[:, begin : begin + half], came).reshape(LEV, count, -1)
            where = slice(first, first + count)
            total[:, where] += local * weight[:, where].astype(F32)


VMEM = pl.BlockSpec(memory_space=pltpu.VMEM)
SMEM = pl.BlockSpec(memory_space=pltpu.SMEM)
HBM = pl.BlockSpec(memory_space=pltpu.HBM)


def call(*args, **kwargs):
    def run(*operands):
        return kernel_call(*args, **kwargs)(*operands)

    return run


def kernel_call(kernel, outs, in_specs, scratch=(), flops=0, limit=24):
    shapes = [jax.ShapeDtypeStruct(shape, kind) for shape, kind in outs]
    many = len(shapes) > 1
    return pl.pallas_call(
        kernel,
        out_shape=shapes if many else shapes[0],
        in_specs=in_specs,
        out_specs=[VMEM] * len(shapes) if many else VMEM,
        scratch_shapes=scratch,
        compiler_params=pltpu.CompilerParams(vmem_limit_bytes=limit << 20),
        cost_estimate=pl.CostEstimate(flops=flops, bytes_accessed=1 << 20, transcendentals=0),
    )


def on_device(
    members,
    control_fine,
    control_mid,
    control_coarse,
    vertical,
    mid_picks,
    coarse_picks,
    band_radii,
):
    devices = lax.axis_size("mem")
    member_total = members.shape[0] * devices
    held = members.shape[0] * LEV
    raw = [
        pltpu.with_memory_space_constraint(c.reshape(held, c.shape[2], c.shape[3]), pltpu.HBM)
        for c in (control_fine, control_mid, control_coarse)
    ]
    members = members.reshape(held * members.shape[2], members.shape[3])
    controls = [c.reshape(held * c.shape[2], c.shape[3]) for c in (control_fine, control_mid, control_coarse)]
    in_hbm = [pltpu.with_memory_space_constraint(c, pltpu.HBM) for c in controls]
    sizes = tuple(c.shape for c in controls)
    all_cells = sum(cells for cells, _ in sizes)
    fine_cells, fine_rows = sizes[0]
    out_cells = fine_cells // 2
    tiles = 4 * held
    span = held * REACH

    edge, odd_main, even_main = call(
        edge_kernel,
        [((REACH, all_cells), B16)] + [((tiles, REACH, 128), B16)] * 2,
        [HBM] * 3,
        [pltpu.VMEM((cells // span, held, REACH, min(rows, 128)), B16) for cells, rows in sizes]
        + [pltpu.VMEM((held, REACH, sizes[2][1]), B16), pltpu.SemaphoreType.DMA((14,))],
        flops=10**7,
    )(*raw)
    count = lax.axis_size("lon")
    odd_pairs = [(i, (i + 1) % count) for i in range(1, count, 2)]
    odd_pairs += [(j, i) for i, j in odd_pairs]
    even_pairs = [(i, i + 1) for i in range(0, count, 2)]
    even_pairs += [(j, i) for i, j in even_pairs]
    arrived = lax.ppermute(edge, "lat", [(0, 1), (1, 0)])
    odd = lax.ppermute(odd_main, "lon", odd_pairs)

    outs = [((cells, fine_rows), F32) for cells, _ in sizes]
    outs += [((rows, fine_rows), B16) for _, rows in sizes]
    outs += [((3, REACH, fine_rows), B16)]
    outs += [((out_cells, cells // 2), B16) for cells, _ in sizes]
    outs += [((LEV * factor * REACH, 2 * LEV * REACH), B16) for factor in FACTORS]
    outs += [((fine_cells, fine_rows), B16)] * 2
    prep = call(
        functools.partial(prep_kernel, sizes),
        outs,
        [SMEM] + [VMEM] * 4 + [HBM] * 3,
        [pltpu.VMEM((256, 256), B16)] + [pltpu.VMEM(s, B16) for s in sizes] + [pltpu.SemaphoreType.DMA((3,))],
        flops=10**9,
    )(band_radii, members, vertical, mid_picks[None], coarse_picks[None], *in_hbm)
    xr, rows, rim, own, side, res = prep[0:3], prep[3:6], prep[6], prep[7:10], prep[10:13], prep[13:15]

    odd_rim, even = call(
        functools.partial(forward_kernel, sizes),
        [((REACH, 3 * span), B16), ((tiles + 3 * span // 128, REACH, 128), B16)],
        [VMEM] * 2,
        flops=10**6,
    )(arrived, even_main)
    odd_rim = lax.ppermute(odd_rim, "lon", odd_pairs)
    even = lax.ppermute(even, "lon", even_pairs)

    partial = call(
        functools.partial(own_kernel, sizes), [((out_cells, fine_rows), F32)], [VMEM] * 11, flops=10**9
    )(arrived, *xr, rim, *own, members, *res)
    field = call(
        functools.partial(side_kernel, sizes),
        [((out_cells, fine_rows), B16)],
        [VMEM] * 15,
        [pltpu.VMEM((LEV, out_cells // LEV, fine_rows), F32)],
        flops=10**9,
    )(
        odd.reshape(tiles * REACH, 128),
        odd_rim,
        even.reshape(-1, 128),
        even,
        *rows,
        rim,
        *side,
        members,
        *res,
        partial,
    )

    blocks = field.reshape(devices, out_cells // devices, fine_rows)
    blocks = lax.all_to_all(blocks, "mem", split_axis=0, concat_axis=0, tiled=True)
    increment = blocks.astype(F32).sum(axis=0) / math.sqrt(member_total - 1)
    return increment[None, :, :]


def solution(mesh):
    placed = (
        P("mem", None, "lon", "lat"),
        P("mem", None, "lon", "lat"),
        P("mem", None, "lon", "lat"),
        P("mem", None, "lon", "lat"),
        P(),
        P(),
        P(),
        P(),
    )
    return jax.shard_map(on_device, mesh=mesh, in_specs=placed, out_specs=P("lon", "mem", "lat"), check_vma=False)
```

```python
import functools
import math

import jax
import jax.numpy as jnp
from jax import lax
from jax.experimental import pallas as pl
from jax.experimental.pallas import tpu as pltpu
from jax.sharding import PartitionSpec as P


REACH = 8
LEV = 16
FACTORS = (1, 2, 4)
B16 = jnp.bfloat16
F32 = jnp.float32


def iota(shape, dim):
    return lax.broadcasted_iota(jnp.int32, shape, dim)


def dot(a, b, ca=1, cb=0):
    return lax.dot_general(a, b, (((ca,), (cb,)), ((), ())), preferred_element_type=F32)


def tap_table(radius):
    lane = iota((8, 128), 1)
    wide = (lane - REACH).astype(F32)
    reach_now = jnp.broadcast_to(radius.astype(F32), wide.shape)
    raw = jnp.exp(-0.5 * jnp.square(wide / (0.5 * reach_now)))
    raw = jnp.where((jnp.abs(wide) <= reach_now) & (lane <= 2 * REACH), raw, 0.0)
    weights = raw / jnp.sum(raw, axis=1, keepdims=True)
    return weights.astype(B16).astype(F32)[0:1]


def taps(offset, table):
    lane = jnp.where(jnp.abs(offset) <= REACH, offset + REACH, 127)
    full = jnp.broadcast_to(table, (offset.shape[0], 128))
    parts = [
        jnp.take_along_axis(full, lane[:, at : at + 128], axis=1, mode="promise_in_bounds")
        for at in range(0, offset.shape[1], 128)
    ]
    return parts[0] if len(parts) == 1 else jnp.concatenate(parts, axis=1)


def edge_kernel(fine, mid, coarse, out, odd, even, buf0, buf1, buf2, buf3, sems):
    low_half = lax.axis_index("lat") == 0
    left_is_odd = lax.axis_index("lon") % 2 == 0
    copies = []

    def begin(source, to):
        copies.append(pltpu.make_async_copy(source, to, sems.at[len(copies)]))
        copies[-1].start()

    held = fine.shape[0]
    first = pl.multiple_of(jnp.where(low_half, fine.shape[2] - 128, 0), 128)
    for ref, buf, lanes in ((coarse, buf2, None), (mid, buf1, None), (fine, buf0, first)):
        for group in range(ref.shape[1] // REACH):
            source = ref.at[:, group * REACH : (group + 1) * REACH]
            if lanes is not None:
                source = ref.at[:, group * REACH : (group + 1) * REACH, pl.ds(lanes, 128)]
            begin(source, buf.at[group])
    for_rows = len(copies)
    begin(coarse, buf3)
    for to, goes_left in ((odd, left_is_odd), (even, jnp.logical_not(left_is_odd))):
        at = 0
        for ref in (fine, mid):
            column = pl.multiple_of(jnp.where(goes_left, 0, ref.shape[1] - REACH), REACH)
            for lane in range(0, ref.shape[2], 128):
                begin(ref.at[:, pl.ds(column, REACH), lane : lane + 128], to.at[at : at + held])
                at += held
    for copy in copies[:for_rows]:
        copy.wait()
    start = 0
    for buf in (buf0, buf1, buf2):
        width = buf.shape[-1]
        base = jnp.where(low_half, width - REACH, 0)
        pick = (iota((REACH, width), 1) == iota((REACH, width), 0) + base).astype(B16)
        cells = buf.shape[0] * held * REACH
        rows = buf[...].astype(F32).reshape(cells, width).astype(B16)
        out[:, start : start + cells] = dot(pick, rows, 1, 1).astype(B16)
        start += cells
    copies[for_rows].wait()
    for to in (odd, even):
        to[3 * held :, :, : buf3.shape[2]] = buf3[...]
    for copy in copies[for_rows + 1 :]:
        copy.wait()


def prep_kernel(
    sizes,
    radii,
    members,
    vertical,
    mid_picks,
    coarse_picks,
    row0,
    row1,
    row2,
    rim,
    own0,
    own1,
    own2,
    side0,
    side1,
    side2,
    res1,
    res2,
    spare,
):
    lat = lax.axis_index("lat")
    lon = lax.axis_index("lon")
    cols = 32
    refs = zip((row0, row1, row2), (own0, own1, own2), (side0, side1, side2))
    for band, (factor, (cells, rows), (row_ref, own_ref, side_ref)) in enumerate(zip(FACTORS, sizes, refs)):
        table = tap_table(radii[band])
        width = cols // factor
        shape = (rows, rows * factor)
        row_ref[...] = taps(iota(shape, 0) - iota(shape, 1) // factor, table).astype(B16)
        base = jnp.where(lat == 0, rows, -REACH)
        shape = (REACH, rows * factor)
        rim[band] = taps(iota(shape, 0) + base - iota(shape, 1) // factor, table).astype(B16)
        reach_cols = factor * REACH
        parts = (
            (own_ref, 0, width, cols, 0, 0),
            (side_ref, 0, REACH, reach_cols, 0, -REACH),
            (side_ref, LEV * REACH, REACH, reach_cols, cols - reach_cols, width),
        )
        for to, at, span, count, first, shift in parts:
            lanes = LEV * span
            place = iota((count, lanes), 1) % span + shift
            target = (iota((count, lanes), 0) + first) // factor
            pattern = taps(place - target, table)
            level = (iota((LEV, lanes), 0) == iota((LEV, lanes), 1) // span).astype(B16)
            spread = dot(vertical[band], level)
            for k in range(LEV):
                to[k * count : (k + 1) * count, at : at + lanes] = (spread[k : k + 1] * pattern).astype(B16)
    full_rows = sizes[0][1]
    block = 8 * cols
    for factor, picks, out in ((2, mid_picks, res1), (4, coarse_picks, res2)):
        rows = full_rows // factor
        width = cols // factor
        total = 2 * rows
        values = jnp.broadcast_to(picks[...].astype(F32), (8, picks.shape[1])).astype(B16)
        if rows == 128:
            along = jnp.where(lat == 0, values[:, :128].astype(F32), values[:, 128:256].astype(F32)).astype(B16)
            start = 0
        else:
            along = values[:, :128]
            start = lat * rows
        shape = (128, full_rows)
        hot = (iota(shape, 0) == start + iota(shape, 1) // factor).astype(B16)
        chosen = dot(along, hot)[0:1].astype(jnp.int32)
        wanted = factor * (iota((1, full_rows), 1) // factor) + chosen
        row_pick = (iota((full_rows, full_rows), 0) == wanted).astype(B16)
        across = values[:, total:]
        shape = (cols, across.shape[1])
        hot = (iota(shape, 1) == lon * width + iota(shape, 0) // factor).astype(B16)
        chosen = dot(hot, across, 1, 1)[:, 0:1].astype(jnp.int32)
        wanted = factor * (iota((cols, 1), 0) // factor) + chosen
        lanes = iota((cols, block), 1)
        for k in range(8):
            spare[k * cols : (k + 1) * cols] = (lanes == wanted + k * cols).astype(B16)
        col_pick = spare[...]
        for part in range(members.shape[0] // block):
            at = slice(part * block, (part + 1) * block)
            by_rows = dot(members[at], row_pick).astype(B16)
            out[at] = dot(col_pick, by_rows).astype(B16)


def forward_kernel(sizes, rim_in, main, odd, even):
    left_is_odd = lax.axis_index("lon") % 2 == 0
    start = 0
    span = main.shape[0] // 4 * REACH
    even[: main.shape[0]] = main[...]
    for band, (cells, rows) in enumerate(sizes):
        for part in range(0, span, 128):
            left = rim_in[:, start + part : start + part + 128]
            right = rim_in[:, start + cells - span + part : start + cells - span + part + 128]
            at = band * span + part
            odd[:, at : at + 128] = jnp.where(left_is_odd, left, right)
            even[main.shape[0] + at // 128] = jnp.where(left_is_odd, right, left)
        start += cells


def own_kernel(
    sizes, rim_in, fine, mid, coarse, row0, row1, row2, rim, own0, own1, own2, members, res1, res2, out
):
    first = True
    start = 0
    held = 2 * LEV
    refs = zip((fine, mid, coarse), (row0, row1, row2), (own0, own1, own2), (members, res1, res2))
    for band, (factor, (cells, rows), (ref, row_ref, own, res)) in enumerate(zip(FACTORS, sizes, refs)):
        width = cells // held
        size = res.shape[0] // 2
        edge = rim[band]
        span = LEV * REACH
        for m in range(2):
            sums = dot(ref[m * cells // 2 : (m + 1) * cells // 2], row_ref[...]).reshape(LEV, width, -1)
            parts = []
            for group in range(width // REACH):
                at = start + (2 * group + m) * span
                parts.append(dot(rim_in[:, at : at + span], edge, 0, 0).reshape(LEV, REACH, -1))
            sums = sums + (parts[0] if len(parts) == 1 else jnp.concatenate(parts, axis=1))
            across = sums.reshape(LEV * width, -1).astype(B16)
            product = dot(own[...], across) * res[m * size : (m + 1) * size].astype(F32)
            out[...] = product if first else out[...] + product
            first = False
        start += cells


def side_kernel(
    sizes,
    odd,
    odd_rim,
    even,
    even_rim,
    row0,
    row1,
    row2,
    rim,
    side0,
    side1,
    side2,
    members,
    res1,
    res2,
    partial,
    out,
    total,
):
    left_is_odd = lax.axis_index("lon") % 2 == 0
    size = members.shape[0] // 2
    cols = total.shape[1]
    span = 2 * LEV * REACH
    half = span // 2
    tiles = even_rim.shape[0] - 6
    at = 3 * span
    order = []
    bands = zip(FACTORS, sizes, (row0, row1, row2), (side0, side1, side2), (members, res1, res2))
    for band, (factor, (cells, rows), row_ref, side, res) in reversed(list(enumerate(bands))):
        both = [0.0, 0.0]
        for lane in reversed(range(0, rows, 128)):
            wide = min(rows, 128)
            one = odd[at : at + span, :wide]
            two = even[at : at + span, :wide]
            at -= span
            matrix = row_ref[lane : lane + wide]
            both[0] += dot(jnp.where(left_is_odd, one, two), matrix)
            both[1] += dot(jnp.where(left_is_odd, two, one), matrix)
        for m in range(2):
            one = odd_rim[:, band * span + m * half : band * span + (m + 1) * half]
            two = even_rim[tiles + 2 * band + m]
            edges = (jnp.where(left_is_odd, one, two), jnp.where(left_is_odd, two, one))
            left, right = [
                (main[m * half : (m + 1) * half] + dot(edge, rim[band], 0, 0)).astype(B16)
                for main, edge in zip(both, edges)
            ]
            order.append((factor, side, res, m, left, right))
    order = order[:1] + order[2:] + order[1:2]
    shape = total.shape
    for step, (factor, side, res, m, left, right) in enumerate(order):
        weight = res[m * size : (m + 1) * size]
        count = factor * REACH
        if count == cols:
            product = dot(side[...], jnp.concatenate([left, right], axis=0)) * weight.astype(F32)
            if step == 0:
                total[...] = (partial[...] + product).reshape(shape)
            else:
                out[...] = (total[...].reshape(out.shape) + product).astype(B16)
            continue
        weight = weight.reshape(shape)
        for begin, first, came in ((0, 0, left), (half, cols - count, right)):
            local = dot(side[:, begin : begin + half], came).reshape(LEV, count, -1)
            where = slice(first, first + count)
            total[:, where] += local * weight[:, where].astype(F32)


VMEM = pl.BlockSpec(memory_space=pltpu.VMEM)
SMEM = pl.BlockSpec(memory_space=pltpu.SMEM)
HBM = pl.BlockSpec(memory_space=pltpu.HBM)


def call(*args, **kwargs):
    def run(*operands):
        return kernel_call(*args, **kwargs)(*operands)

    return run


def kernel_call(kernel, outs, in_specs, scratch=(), flops=0, limit=24):
    shapes = [jax.ShapeDtypeStruct(shape, kind) for shape, kind in outs]
    many = len(shapes) > 1
    return pl.pallas_call(
        kernel,
        out_shape=shapes if many else shapes[0],
        in_specs=in_specs,
        out_specs=[VMEM] * len(shapes) if many else VMEM,
        scratch_shapes=scratch,
        compiler_params=pltpu.CompilerParams(vmem_limit_bytes=limit << 20),
        cost_estimate=pl.CostEstimate(flops=flops, bytes_accessed=1 << 20, transcendentals=0),
    )


def on_device(
    members,
    control_fine,
    control_mid,
    control_coarse,
    vertical,
    mid_picks,
    coarse_picks,
    band_radii,
):
    devices = lax.axis_size("mem")
    member_total = members.shape[0] * devices
    held = members.shape[0] * LEV
    raw = [
        pltpu.with_memory_space_constraint(c.reshape(held, c.shape[2], c.shape[3]), pltpu.HBM)
        for c in (control_fine, control_mid, control_coarse)
    ]
    members = members.reshape(held * members.shape[2], members.shape[3])
    controls = [c.reshape(held * c.shape[2], c.shape[3]) for c in (control_fine, control_mid, control_coarse)]
    sizes = tuple(c.shape for c in controls)
    all_cells = sum(cells for cells, _ in sizes)
    fine_cells, fine_rows = sizes[0]
    out_cells = fine_cells // 2
    tiles = 4 * held
    span = held * REACH

    edge, odd_main, even_main = call(
        edge_kernel,
        [((REACH, all_cells), B16)] + [((tiles, REACH, 128), B16)] * 2,
        [HBM] * 3,
        [pltpu.VMEM((cells // span, held, REACH, min(rows, 128)), B16) for cells, rows in sizes]
        + [pltpu.VMEM((held, REACH, sizes[2][1]), B16), pltpu.SemaphoreType.DMA((14,))],
        flops=10**7,
    )(*raw)
    count = lax.axis_size("lon")
    odd_pairs = [(i, (i + 1) % count) for i in range(1, count, 2)]
    odd_pairs += [(j, i) for i, j in odd_pairs]
    even_pairs = [(i, i + 1) for i in range(0, count, 2)]
    even_pairs += [(j, i) for i, j in even_pairs]
    arrived = lax.ppermute(edge, "lat", [(0, 1), (1, 0)])
    odd = lax.ppermute(odd_main, "lon", odd_pairs)

    outs = [((rows, fine_rows), B16) for _, rows in sizes]
    outs += [((3, REACH, fine_rows), B16)]
    outs += [((out_cells, cells // 2), B16) for cells, _ in sizes]
    outs += [((LEV * factor * REACH, 2 * LEV * REACH), B16) for factor in FACTORS]
    outs += [((fine_cells, fine_rows), B16)] * 2
    prep = call(
        functools.partial(prep_kernel, sizes), outs, [SMEM] + [VMEM] * 4, [pltpu.VMEM((256, 256), B16)], flops=10**9
    )(band_radii, members, vertical, mid_picks[None], coarse_picks[None])
    rows, rim, own, side, res = prep[0:3], prep[3], prep[4:7], prep[7:10], prep[10:12]

    odd_rim, even = call(
        functools.partial(forward_kernel, sizes),
        [((REACH, 3 * span), B16), ((tiles + 3 * span // 128, REACH, 128), B16)],
        [VMEM] * 2,
        flops=10**6,
    )(arrived, even_main)
    odd_rim = lax.ppermute(odd_rim, "lon", odd_pairs)
    even = lax.ppermute(even, "lon", even_pairs)

    partial = call(
        functools.partial(own_kernel, sizes), [((out_cells, fine_rows), F32)], [VMEM] * 14, flops=10**9
    )(arrived, *controls, *rows, rim, *own, members, *res)
    field = call(
        functools.partial(side_kernel, sizes),
        [((out_cells, fine_rows), B16)],
        [VMEM] * 15,
        [pltpu.VMEM((LEV, out_cells // LEV, fine_rows), F32)],
        flops=10**9,
    )(
        odd.reshape(tiles * REACH, 128),
        odd_rim,
        even.reshape(-1, 128),
        even,
        *rows,
        rim,
        *side,
        members,
        *res,
        partial,
    )

    blocks = field.reshape(devices, out_cells // devices, fine_rows)
    blocks = lax.all_to_all(blocks, "mem", split_axis=0, concat_axis=0, tiled=True)
    increment = blocks.astype(F32).sum(axis=0) / math.sqrt(member_total - 1)
    return increment[None, :, :]


def solution(mesh):
    placed = (
        P("mem", None, "lon", "lat"),
        P("mem", None, "lon", "lat"),
        P("mem", None, "lon", "lat"),
        P("mem", None, "lon", "lat"),
        P(),
        P(),
        P(),
        P(),
    )
    return jax.shard_map(on_device, mesh=mesh, in_specs=placed, out_specs=P("lon", "mem", "lat"), check_vma=False)
```
